32 devices in a mesh: groups: 2 (over y), seq: 16 (over z, x, core).
Axes of the slice: x: 2, y: 2, z: 4, core: 2. Of those that a mesh axis runs over, the one named last changes fastest.
Arguments:
- queries: bfloat16 [8192, 768], P(('groups', 'seq')), parts along dimension 0, may hold values from -30 to 30
- keys: bfloat16 [8192, 128], P(('groups', 'seq')), parts along dimension 0, may hold values from -14 to 14
- values: bfloat16 [8192, 128], P(('groups', 'seq')), parts along dimension 0, may hold values from -6 to 6
- span_ids: int32 [64], P(('groups', 'seq')), parts along dimension 0, may hold values from 0 to 31, each once
- lengths: int32 [16], P('groups'), parts along dimension 0, may hold values from 1 to 16, 32 in all
- page_dest: int32 [64], P('groups'), parts along dimension 0, may hold values from 0 to 31, each once
Outputs:
- context: bfloat16 [8192, 768], P(('groups', 'seq')), parts along dimension 0
- paged_kv: bfloat16 [64, 128, 256], P(('groups', 'seq')), parts along dimension 0
The draws below stay inside these ranges and needn't reach their ends.
There are 2 independent parts, one for each index of `groups`. The reference program is written for one: setup_inputs(seed, part) draws one part's arguments, and reference() takes and returns one part's arrays. A program takes and returns all parts, laid end to end along the dimension named above; each array names one. Nothing has to cross between parts.
Inputs may be any that keep to these rules, and one draw needn't show every extreme that they name: `span_ids`: every packed span number appears once over the whole array. The lengths sum to 32, and one of them equals 16. `page_dest`: every page slot receives exactly one span.
All inputs are finite; a program needn't handle non-finite values.
Results may differ from the reference program's by a relative error of at most 0.012.
The reference program's roundings to bfloat16 on the way count: a program that leaves them out, or rounds other values in their place, can miss the bound.
Values may be sent and summed in bfloat16 or wider, within the bound.
No kernel may reach another device: no remote copies, remote signals or barrier semaphores. Data moves between devices by JAX's collectives and lax.ppermute only.
A program may use at most 128 MiB of HBM per device.

```python
import math
import jax
import jax.numpy as jnp
import numpy as np
from jax import lax

HD = 128
QH = 6
SPAN = 128
NSEQ = 8
SPANS = 32
TOKENS = 4096
MOST = 16


def draw_queries(key, part):
    inner = jax.random.fold_in(key, 101)
    base = jnp.clip(3.0 * jax.random.normal(inner, (TOKENS, QH * HD), jnp.float32), -15.0, 15.0)
    return base.astype(jnp.bfloat16)


def draw_keys(key, part):
    inner = jax.random.fold_in(key, 202)
    base = jnp.clip(jax.random.normal(inner, (TOKENS, HD), jnp.float32), -4.0, 4.0)
    return base.astype(jnp.bfloat16)


def steps_of(own_key, shape, pieces, smallest, largest):
    gain, own = 1.0, jax.random.fold_in(own_key, 6)
    for axis_at, shards_of in pieces:
        draws = jnp.exp(jax.random.uniform(jax.random.fold_in(own, axis_at), (shards_of,), jnp.float32, smallest / len(pieces), largest / len(pieces)))
        gain = gain * jnp.repeat(draws, shape[axis_at] // shards_of).reshape([-1 if axis == axis_at else 1 for axis in range(len(shape))])
    return gain


def profile(number_of, total, bound, slope):
    weights = [(1 << 20) // math.isqrt(standing ** slope) + 1 for standing in range(2, number_of + 1)]
    rest, counts = total - bound - (number_of - 1), [1] * (number_of - 1)
    while rest > 0:
        free = [i for i in range(number_of - 1) if counts[i] < bound]
        pool, remaining = sum([weights[i] for i in free]), rest
        for i in free:
            addition = min(bound - counts[i], max(1, remaining * weights[i] // pool), rest)
            counts[i] = counts[i] + addition
            rest = rest - addition
    return np.array([bound] + counts)


def uneven(stream_key, amount, total, most, skew):
    if amount == 2:
        one = jax.random.randint(stream_key, (), max(1, total - most), min(most, total - 1) + 1)
        return jnp.stack([one, total - one])
    sizes = jnp.asarray(profile(amount, total, most, skew), jnp.int32)
    couples = (amount - 1) // 2
    source_of, sink = sizes[1:1 + 2 * couples:2], sizes[2:2 + 2 * couples:2]
    room = jnp.minimum(source_of - 1, most - sink)
    shifted = jax.random.randint(jax.random.fold_in(stream_key, 1), (couples,), 0, 1 << 20) % (room + 1)
    sizes = sizes.at[1:1 + 2 * couples:2].set(source_of - shifted).at[2:2 + 2 * couples:2].set(sink + shifted)
    return sizes[jax.random.permutation(jax.random.fold_in(stream_key, 2), amount)]


def gaussian(rng, extent, scale, most, split=(), kind=jnp.bfloat16):
    gain = steps_of(rng, extent, split, -0.22, 0.18) if split else 1.0
    result = jax.random.normal(rng, extent, jnp.float32) * scale * gain
    return jnp.minimum(jnp.maximum(result, -most), most).astype(kind)


def setup_inputs(seed: int = 0, part: int = 0) -> dict:
    streams_of = jax.random.split(jax.random.key(seed), 7)
    part_splits = jax.random.split(jax.random.fold_in(streams_of[6], part), 7)
    return {
        "queries": draw_queries(jax.random.fold_in(jax.random.fold_in(streams_of[6], part), 71), part),
        "keys": draw_keys(jax.random.fold_in(jax.random.fold_in(streams_of[6], part), 71), part),
        "values": gaussian(part_splits[2], (TOKENS, HD), 1.0, 6.0, ((0, 16),)),
        "span_ids": jax.random.permutation(part_splits[3], SPANS).astype(jnp.int32),
        "lengths": uneven(part_splits[4], NSEQ, SPANS, MOST, 2).astype(jnp.int32),
        "page_dest": jax.random.permutation(part_splits[5], SPANS).astype(jnp.int32),
    }


THETA = 1000000.0
NEG = -1e30


def rotate(x, pos):
    half = HD // 2
    freq = THETA ** (-(jnp.arange(half, dtype=jnp.float32) * 2.0 / HD))
    angle = pos[:, None] * freq[None, :]
    cosine = jnp.cos(angle)[:, None, :]
    sine = jnp.sin(angle)[:, None, :]
    first = x[..., :half]
    second = x[..., half:]
    return jnp.concatenate([first * cosine - second * sine, second * cosine + first * sine], axis=-1)


def locate(tokens, lengths):
    span_of = tokens // SPAN
    ends = jnp.cumsum(lengths)
    start_span = jnp.sum(jnp.where(ends[None, :] <= span_of[:, None], lengths[None, :], 0), axis=1)
    start = (start_span * SPAN).astype(jnp.int32)
    return start, (tokens - start).astype(jnp.int32)


def reference(queries, keys, values, span_ids, lengths, page_dest):
    rows = jnp.arange(TOKENS, dtype=jnp.int32)
    tokens = (span_ids[rows // SPAN] * SPAN + rows % SPAN).astype(jnp.int32)
    start, pos = locate(tokens, lengths)
    posf = pos.astype(jnp.float32)
    q_rot = rotate(queries.astype(jnp.float32).reshape(TOKENS, QH, HD), posf).astype(jnp.bfloat16)
    k_rot = rotate(keys.astype(jnp.float32)[:, None, :], posf)[:, 0, :].astype(jnp.bfloat16)
    q_blocks = q_rot.reshape(SPANS, SPAN * QH, HD)
    q_tok = jnp.repeat(tokens, QH).reshape(SPANS, SPAN * QH)
    q_start = jnp.repeat(start, QH).reshape(SPANS, SPAN * QH)
    scale = 1.0 / (HD ** 0.5)

    def one_span(item):
        block, qtok, qstart = item
        scores = jnp.dot(block, k_rot.T, preferred_element_type=jnp.float32) * scale
        mask = (tokens[None, :] <= qtok[:, None]) & (tokens[None, :] >= qstart[:, None])
        best = jnp.max(jnp.where(mask, scores, NEG), axis=1)
        weights = jnp.where(mask, jnp.exp(scores - best[:, None]), 0.0)
        total = jnp.sum(weights, axis=1)
        mixed = jnp.dot(weights.astype(jnp.bfloat16), values, preferred_element_type=jnp.float32)
        return (mixed / total[:, None]).astype(jnp.bfloat16)

    context = lax.map(one_span, (q_blocks, q_tok, q_start)).reshape(TOKENS, QH * HD)
    packed = jnp.concatenate([k_rot, values], axis=1).reshape(SPANS, SPAN, 2 * HD)
    slots = page_dest[span_ids].astype(jnp.int32)
    paged_kv = jnp.zeros((SPANS, SPAN, 2 * HD), jnp.bfloat16).at[slots].set(packed)
    return context, paged_kv
```

```python
import functools
import math

import jax
import jax.numpy as jnp
import numpy as np
from jax import lax
from jax.experimental import pallas as pl
from jax.experimental.pallas import tpu as pltpu
from jax.sharding import PartitionSpec as P


HD = 128
QH = 6
SPAN = 128
THETA = 1000000.0
NEG = -1e30
META = 8
SCALE = math.log2(math.e) / math.sqrt(HD)


def tables(spans):
    half = HD // 2
    freq = THETA ** (-(np.arange(half, dtype=np.float64) * 2.0 / HD))
    at = np.concatenate([SPAN * np.arange(spans), np.arange(SPAN)]).astype(np.float64)
    angle = at[:, None] * freq[None, :]
    cosine, sine = np.cos(angle), np.sin(angle)
    return (
        np.concatenate([cosine, cosine], axis=1).astype(np.float32),
        np.concatenate([-sine, sine], axis=1).astype(np.float32),
    )


def history(span, lengths_ref):
    start = jnp.int32(0)
    end = jnp.int32(0)
    for i in range(lengths_ref.shape[0]):
        end = end + lengths_ref[i]
        start = jnp.where(end <= span, end, start)
    return start


def turn(cos_ref, sin_ref, spans, depth):
    cos_a, sin_a = cos_ref[pl.ds(depth, 1), :], sin_ref[pl.ds(depth, 1), :]
    cos_b, sin_b = cos_ref[spans : spans + SPAN, :], sin_ref[spans : spans + SPAN, :]
    return cos_a * cos_b - sin_a * sin_b, sin_a * cos_b + cos_a * sin_b


def rotary(x, cosine, sine):
    x = x.astype(jnp.float32)
    return (x * cosine + pltpu.roll(x, HD // 2, 1) * sine).astype(jnp.bfloat16)


def fetch_all(pairs, sems):
    copies = [pltpu.make_async_copy(a, b, sems.at[i]) for i, (a, b) in enumerate(pairs)]
    for copy in copies:
        copy.start()
    return copies


def prepare(spans, *refs):
    out_ref = refs[6]
    ids_ref, lengths_ref, keys_ref, values_ref, cos_ref, sin_ref, sems = refs[7:]
    for copy in fetch_all(list(zip(refs[:6], refs[7:13])), sems):
        copy.wait()
    rows = keys_ref.shape[0]
    row = lax.broadcasted_iota(jnp.int32, (META, HD), 0)
    meta = jnp.zeros((META, HD), jnp.float32)
    for i in range(rows // SPAN):
        span = ids_ref[i]
        cosine, sine = turn(cos_ref, sin_ref, spans, span - history(span, lengths_ref))
        own = slice(i * SPAN, (i + 1) * SPAN)
        out_ref[own, :] = rotary(keys_ref[own, :], cosine, sine)
        meta = jnp.where(row == i, span.astype(jnp.float32), meta)
    out_ref[rows : 2 * rows, :] = values_ref[...]
    out_ref[2 * rows :, :] = meta.astype(jnp.bfloat16)


LADDER = (4, 2, 1)


def lanes(x, combine):
    parts = [x[:, i : i + HD] for i in range(0, x.shape[1], HD)]
    while len(parts) > 1:
        parts = [combine(*parts[i : i + 2]) if i + 1 < len(parts) else parts[i] for i in range(0, len(parts), 2)]
    return parts[0]


def scores_of(queries, keys):
    return lax.dot_general(
        queries, keys, (((1,), (1,)), ((), ())), preferred_element_type=jnp.float32
    )


def attend(queries, keys, values, old, old_total, old_accum, mask=None):
    scores = lax.dot_general(
        queries, keys, (((1,), (1,)), ((), ())), preferred_element_type=jnp.float32
    )
    if mask is not None:
        scores = jnp.where(mask, scores, NEG)
    top = jnp.max(lanes(scores, jnp.maximum), axis=1, keepdims=True)
    top = jnp.broadcast_to(top, (queries.shape[0], HD))
    if old is not None:
        top = jnp.maximum(old, top)
    weights = jnp.exp2((scores - jnp.tile(top, (1, keys.shape[0] // HD))) * SCALE)
    total = lanes(weights, jnp.add)
    accum = jnp.dot(weights.astype(jnp.bfloat16), values, preferred_element_type=jnp.float32)
    if old is not None:
        factor = jnp.exp2((old - top) * SCALE)
        total = total + old_total * factor
        accum = accum + old_accum * factor
    return top, total, accum


def early(spans, *refs):
    q_rot, best, total, accum = refs[6:10]
    ids_ref, lengths_ref, queries_ref, cos_ref, sin_ref, sems = refs[10:]
    own_ref = refs[5]
    for copy in fetch_all(list(zip(refs[:5], refs[10:15])), sems):
        copy.wait()
    tok = queries_ref.shape[0]
    rows = QH * SPAN
    row = lax.broadcasted_iota(jnp.int32, (rows, SPAN), 0) % SPAN
    key = lax.broadcasted_iota(jnp.int32, (rows, SPAN), 1)
    causal = key <= row
    for s in range(tok // SPAN):
        span = ids_ref[s]
        cosine, sine = turn(cos_ref, sin_ref, spans, span - history(span, lengths_ref))
        for h in range(QH):
            q_rot[s * rows + h * SPAN : s * rows + (h + 1) * SPAN, :] = rotary(
                queries_ref[s * SPAN : (s + 1) * SPAN, h * HD : (h + 1) * HD], cosine, sine
            )
        keys = own_ref[s * SPAN : (s + 1) * SPAN, :]
        values = own_ref[tok + s * SPAN : tok + (s + 1) * SPAN, :]
        own = slice(s * rows, (s + 1) * rows)
        best[own, :], total[own, :], accum[own, :] = attend(
            q_rot[own, :], keys, values, None, None, None, causal
        )


def absorb(
    per_rank, count, last, first_page_ref, ids_ref, lengths_ref, dest_ref, q_rot, best_in, total_in, accum_in, *rest
):
    pieces, rest = rest[:count], rest[count:]
    if last:
        _, context_ref, pages_ref, best, total, accum, rows_out = rest[:7]
        rest = rest[7:]
    else:
        best, total, accum, pages_ref = rest[:4]
        rest = rest[4:]
    kv, page, ids_vmem, where, ids_smem, id_sem, page_sem, out_sem = rest
    tok = per_rank * SPAN
    rows = QH * SPAN
    block = 2 * tok + META

    lane = lax.broadcasted_iota(jnp.int32, (META, HD), 1)
    blocks = [(p, base) for p in pieces for base in range(0, p.shape[0], block)]
    for group in range(ids_vmem.shape[0]):
        found = jnp.zeros((META, HD), jnp.float32)
        for i in range(group * HD, min((group + 1) * HD, len(blocks))):
            piece, base = blocks[i]
            meta = piece[base + 2 * tok : base + block, :].astype(jnp.float32)
            found = jnp.where(lane == i - group * HD, meta, found)
        ids_vmem[group] = found.astype(jnp.int32)
    fetch = pltpu.make_async_copy(ids_vmem, ids_smem, id_sem)
    fetch.start()

    for i, (piece, base) in enumerate(blocks):
        kv[2 * tok * i : 2 * tok * (i + 1), :] = piece[base : base + 2 * tok, :]
    best[...] = best_in[...]
    total[...] = total_in[...]
    accum[...] = accum_in[...]

    own_ids = [ids_ref[s] for s in range(per_rank)]
    starts = [history(span, lengths_ref) for span in own_ids]
    first_page = first_page_ref[0]
    fetch.wait()

    def note(i, found):
        found = list(found)
        for j in range(per_rank):
            number = ids_smem[i // HD, j, i % HD]
            place = (2 * i * per_rank + j) * SPAN
            for s in range(per_rank):
                where[s, found[s]] = place
                seen = (number >= starts[s]) & (number < own_ids[s])
                found[s] = found[s] + seen.astype(jnp.int32)
            to = dest_ref[number] - first_page
            for p in range(per_rank):
                found[per_rank + p] = jnp.where(to == p, place, found[per_rank + p])
        return tuple(found)

    found = (jnp.int32(0),) * per_rank + (jnp.int32(-1),) * per_rank
    found = lax.fori_loop(0, len(blocks), note, found, unroll=len(blocks) <= 16)

    def tile(place):
        return kv[pl.ds(pl.multiple_of(place, SPAN), SPAN), :]

    def page_copy(p):
        return pltpu.make_async_copy(page.at[p], pages_ref.at[p], page_sem.at[p])

    for p in range(per_rank):

        @pl.when(found[per_rank + p] >= 0)
        def _():
            page[p, :, :HD] = tile(found[per_rank + p])
            page[p, :, HD:] = tile(found[per_rank + p] + tok)
            page_copy(p).start()

    def step(s, places):
        keys = jnp.concatenate([tile(p) for p in places], axis=0)
        values = jnp.concatenate([tile(p + tok) for p in places], axis=0)
        own = slice(s * rows, (s + 1) * rows)
        scores = scores_of(q_rot[own, :], keys)
        old = best[own, :]
        top = jnp.maximum(old, jnp.max(scores, axis=1, keepdims=True))
        factor = jnp.exp2((old - top) * SCALE)
        weights = jnp.exp2((scores - jnp.tile(top, (1, len(places)))) * SCALE)
        best[own, :] = top
        total[own, :] = total[own, :] * factor + lanes(weights, jnp.add)
        accum[own, :] = accum[own, :] * factor + jnp.dot(
            weights.astype(jnp.bfloat16), values, preferred_element_type=jnp.float32
        )

    outs = []
    for s in range(per_rank):
        seen = found[s]

        @pl.loop(0, seen // LADDER[0])
        def _(b):
            step(s, [where[s, LADDER[0] * b + i] for i in range(LADDER[0])])

        for size in LADDER[1:]:

            @pl.when(seen % (2 * size) >= size)
            def _():
                base = seen // (2 * size) * (2 * size)
                step(s, [where[s, base + i] for i in range(size)])

        if last:
            own = slice(s * SPAN, (s + 1) * SPAN)
            for h in range(QH):
                part = slice(s * rows + h * SPAN, s * rows + (h + 1) * SPAN)
                rows_out[own, h * HD : (h + 1) * HD] = (
                    accum[part, :] / jnp.sum(total[part, :], axis=1, keepdims=True)
                ).astype(jnp.bfloat16)
            outs.append(pltpu.make_async_copy(rows_out.at[own, :], context_ref.at[own, :], out_sem.at[s]))
            outs[-1].start()

    for copy in outs:
        copy.wait()
    for p in range(per_rank):

        @pl.when(found[per_rank + p] >= 0)
        def _():
            page_copy(p).wait()


SMEM = pl.BlockSpec(memory_space=pltpu.SMEM)
VMEM = pl.BlockSpec(memory_space=pltpu.VMEM)
ANY = pl.BlockSpec(memory_space=pltpu.HBM)
LIMIT = pltpu.CompilerParams(vmem_limit_bytes=24 << 20)


def vmem(x):
    return pltpu.with_memory_space_constraint(x, pltpu.VMEM)


def hbm(x):
    return pltpu.with_memory_space_constraint(x, pltpu.HBM)


ROUTE = (
    ("A", "o", 8),
    ("B", "o", 4),
    ("X", "o", 2),
    ("co", "o", 1),
    ("BA", "A", 4),
    ("XB", "B", 2),
    ("XA", "A", 2),
    ("cX", "X", 1),
    ("cA", "A", 1),
    ("cB", "B", 1),
    ("XBA", "BA", 2),
    ("cBA", "BA", 1),
    ("cXB", "XB", 1),
    ("cXA", "XA", 1),
    ("cXBA", "XBA", 1),
)
SOON = ("o", "X", "B", "A", "BA", "co", "cX", "cB", "cA")
LATE = ("cBA", "XB", "XA", "cXB", "cXA", "XBA", "cXBA")


def on_device(ranks, queries, keys, values, span_ids, lengths, page_dest):
    return plan(ranks, queries, keys, values, span_ids, lengths, page_dest)


def plan(ranks, queries, keys, values, span_ids, lengths, page_dest):
    tok = queries.shape[0]
    per_rank = span_ids.shape[0]
    spans = page_dest.shape[0]
    block = 2 * tok + META
    rows = per_rank * QH * SPAN
    cosine, sine = (jnp.asarray(t) for t in tables(spans))
    ints = [pltpu.SMEM(x.shape, x.dtype) for x in (span_ids, lengths)]
    turns = [pltpu.VMEM(x.shape, x.dtype) for x in (cosine, sine)]
    packed = pl.pallas_call(
        functools.partial(prepare, spans),
        out_shape=pltpu.VMEM((block, HD), jnp.bfloat16),
        in_specs=[ANY] * 6,
        out_specs=VMEM,
        scratch_shapes=ints
        + [pltpu.VMEM(x.shape, x.dtype) for x in (keys, values)]
        + turns
        + [pltpu.SemaphoreType.DMA((6,))],
        compiler_params=LIMIT,
        name="prepare",
    )(*map(hbm, (span_ids, lengths, keys, values, cosine, sine)))

    def swap(x, distance):
        return lax.ppermute(x, "seq", [(i, i ^ distance) for i in range(ranks)])

    own = packed
    distance = ranks // 2
    while distance >= 16:
        own = jnp.concatenate([own, swap(own, distance)], axis=0)
        distance //= 2
    held = {"o": own}
    for name, source, distance in ROUTE:
        held[name] = swap(held[source], distance)

    state_shapes = tuple(pltpu.VMEM((rows, n), jnp.float32) for n in (HD, HD, HD))
    q_rot, *state = pl.pallas_call(
        functools.partial(early, spans),
        out_shape=(pltpu.VMEM((rows, HD), jnp.bfloat16), *state_shapes),
        in_specs=[ANY] * 5 + [VMEM],
        out_specs=(VMEM,) * 4,
        scratch_shapes=ints
        + [pltpu.VMEM(queries.shape, queries.dtype)]
        + turns
        + [pltpu.SemaphoreType.DMA((5,))],
        compiler_params=LIMIT,
        name="early",
    )(*map(hbm, (span_ids, lengths, queries, cosine, sine)), vmem(packed))

    first_page = (lax.axis_index("seq") * per_rank).astype(jnp.int32).reshape(1)
    pages_shape = jax.ShapeDtypeStruct((per_rank, SPAN, 2 * HD), jnp.bfloat16)

    def take(names, last, state, pages):
        pieces = [vmem(held[n]) for n in names]
        length = sum(p.shape[0] for p in pieces)
        units = length // block
        lane_groups = -(-units // HD)
        scratch = [
            pltpu.VMEM((units * 2 * tok, HD), jnp.bfloat16),
            pltpu.VMEM((per_rank, SPAN, 2 * HD), jnp.bfloat16),
            pltpu.VMEM((lane_groups, META, HD), jnp.int32),
            pltpu.SMEM((per_rank, units * per_rank + 4), jnp.int32),
            pltpu.SMEM((lane_groups, META, HD), jnp.int32),
            pltpu.SemaphoreType.DMA,
            pltpu.SemaphoreType.DMA((per_rank,)),
            pltpu.SemaphoreType.DMA((per_rank,)),
        ]
        if last:
            out_shape = (jax.ShapeDtypeStruct((tok, QH * HD), jnp.bfloat16), pages_shape)
            out_specs = (ANY, ANY)
            scratch = [
                *state_shapes,
                pltpu.VMEM((tok, QH * HD), jnp.bfloat16),
            ] + scratch
        else:
            out_shape = (*state_shapes, pages_shape)
            out_specs = (VMEM,) * 3 + (ANY,)
        inputs = [first_page, span_ids, lengths, page_dest, vmem(q_rot), *map(vmem, state), *pieces]
        in_specs = [SMEM] * 4 + [VMEM] * (4 + len(pieces))
        aliases = {}
        if last:
            aliases = {len(inputs): 1}
            inputs.append(pages)
            in_specs.append(ANY)
        return pl.pallas_call(
            functools.partial(absorb, per_rank, len(pieces), last),
            out_shape=out_shape,
            in_specs=in_specs,
            out_specs=out_specs,
            scratch_shapes=scratch,
            input_output_aliases=aliases,
            compiler_params=LIMIT,
            name="late" if last else "soon",
        )(*inputs)

    *state, pages = take(SOON, False, state, None)
    context, pages = take(LATE, True, state, pages)
    return context, pages


def solution(mesh):
    return jax.shard_map(
        functools.partial(on_device, mesh.shape["seq"]),
        mesh=mesh,
        in_specs=(
            P(("groups", "seq"), None),
            P(("groups", "seq"), None),
            P(("groups", "seq"), None),
            P(("groups", "seq")),
            P("groups"),
            P("groups"),
        ),
        out_specs=(P(("groups", "seq"), None), P(("groups", "seq"), None, None)),
        check_vma=False,
    )
```

```python
import functools
import math

import jax
import jax.numpy as jnp
import numpy as np
from jax import lax
from jax.experimental import pallas as pl
from jax.experimental.pallas import tpu as pltpu
from jax.sharding import PartitionSpec as P


HD = 128
QH = 6
SPAN = 128
THETA = 1000000.0
NEG = -1e30
META = 8
SCALE = math.log2(math.e) / math.sqrt(HD)


def tables(spans):
    half = HD // 2
    freq = THETA ** (-(np.arange(half, dtype=np.float64) * 2.0 / HD))
    at = np.concatenate([SPAN * np.arange(spans), np.arange(SPAN)]).astype(np.float64)
    angle = at[:, None] * freq[None, :]
    cosine, sine = np.cos(angle), np.sin(angle)
    return (
        np.concatenate([cosine, cosine], axis=1).astype(np.float32),
        np.concatenate([-sine, sine], axis=1).astype(np.float32),
    )


def history(span, lengths_ref):
    start = jnp.int32(0)
    end = jnp.int32(0)
    for i in range(lengths_ref.shape[0]):
        end = end + lengths_ref[i]
        start = jnp.where(end <= span, end, start)
    return start


def turn(cos_ref, sin_ref, spans, depth):
    cos_a, sin_a = cos_ref[pl.ds(depth, 1), :], sin_ref[pl.ds(depth, 1), :]
    cos_b, sin_b = cos_ref[spans : spans + SPAN, :], sin_ref[spans : spans + SPAN, :]
    return cos_a * cos_b - sin_a * sin_b, sin_a * cos_b + cos_a * sin_b


def rotary(x, cosine, sine):
    x = x.astype(jnp.float32)
    return (x * cosine + pltpu.roll(x, HD // 2, 1) * sine).astype(jnp.bfloat16)


def fetch_all(pairs, sems):
    copies = [pltpu.make_async_copy(a, b, sems.at[i]) for i, (a, b) in enumerate(pairs)]
    for copy in copies:
        copy.start()
    return copies


def prepare(spans, *refs):
    out_ref = refs[6]
    ids_ref, lengths_ref, keys_ref, values_ref, cos_ref, sin_ref, sems = refs[7:]
    for copy in fetch_all(list(zip(refs[:6], refs[7:13])), sems):
        copy.wait()
    rows = keys_ref.shape[0]
    row = lax.broadcasted_iota(jnp.int32, (META, HD), 0)
    meta = jnp.zeros((META, HD), jnp.float32)
    for i in range(rows // SPAN):
        span = ids_ref[i]
        cosine, sine = turn(cos_ref, sin_ref, spans, span - history(span, lengths_ref))
        own = slice(i * SPAN, (i + 1) * SPAN)
        out_ref[own, :] = rotary(keys_ref[own, :], cosine, sine)
        meta = jnp.where(row == i, span.astype(jnp.float32), meta)
    out_ref[rows : 2 * rows, :] = values_ref[...]
    out_ref[2 * rows :, :] = meta.astype(jnp.bfloat16)


LADDER = (4, 2, 1)


def lanes(x, combine):
    parts = [x[:, i : i + HD] for i in range(0, x.shape[1], HD)]
    while len(parts) > 1:
        parts = [combine(*parts[i : i + 2]) if i + 1 < len(parts) else parts[i] for i in range(0, len(parts), 2)]
    return parts[0]


def scores_of(queries, keys):
    return lax.dot_general(
        queries, keys, (((1,), (1,)), ((), ())), preferred_element_type=jnp.float32
    )


def attend(queries, keys, values, old, old_total, old_accum, mask=None):
    scores = lax.dot_general(
        queries, keys, (((1,), (1,)), ((), ())), preferred_element_type=jnp.float32
    )
    if mask is not None:
        scores = jnp.where(mask, scores, NEG)
    top = jnp.max(lanes(scores, jnp.maximum), axis=1, keepdims=True)
    top = jnp.broadcast_to(top, (queries.shape[0], HD))
    if old is not None:
        top = jnp.maximum(old, top)
    weights = jnp.exp2((scores - jnp.tile(top, (1, keys.shape[0] // HD))) * SCALE)
    total = lanes(weights, jnp.add)
    accum = jnp.dot(weights.astype(jnp.bfloat16), values, preferred_element_type=jnp.float32)
    if old is not None:
        factor = jnp.exp2((old - top) * SCALE)
        total = total + old_total * factor
        accum = accum + old_accum * factor
    return top, total, accum


def early(spans, *refs):
    own_ref = refs[5]
    q_rot, best, total, accum = refs[6:10]
    ids_ref, lengths_ref, queries_ref, cos_ref, sin_ref, sems = refs[10:]
    for copy in fetch_all(list(zip(refs[:5], refs[10:15])), sems):
        copy.wait()
    tok = queries_ref.shape[0]
    rows = QH * SPAN
    row = lax.broadcasted_iota(jnp.int32, (rows, SPAN), 0) % SPAN
    key = lax.broadcasted_iota(jnp.int32, (rows, SPAN), 1)
    causal = key <= row
    for s in range(tok // SPAN):
        span = ids_ref[s]
        cosine, sine = turn(cos_ref, sin_ref, spans, span - history(span, lengths_ref))
        for h in range(QH):
            q_rot[s * rows + h * SPAN : s * rows + (h + 1) * SPAN, :] = rotary(
                queries_ref[s * SPAN : (s + 1) * SPAN, h * HD : (h + 1) * HD], cosine, sine
            )
        keys = own_ref[s * SPAN : (s + 1) * SPAN, :]
        values = own_ref[tok + s * SPAN : tok + (s + 1) * SPAN, :]
        own = slice(s * rows, (s + 1) * rows)
        best[own, :], total[own, :], accum[own, :] = attend(
            q_rot[own, :], keys, values, None, None, None, causal
        )


def absorb(
    per_rank, count, last, ids_hbm, lengths_hbm, dest_hbm, q_rot, best_in, total_in, accum_in, *rest
):
    pieces, rest = rest[:count], rest[count:]
    if last:
        _, best, total, accum, context_ref, pages_ref, rows_out = rest[:7]
        rest = rest[7:]
    else:
        best, total, accum, pages_ref = rest[:4]
        rest = rest[4:]
    kv, page, ids_vmem, where, ids_smem, ids_ref, lengths_ref, dest_ref, in_sem, id_sem, page_sem, out_sem = rest
    ints = fetch_all([(ids_hbm, ids_ref), (lengths_hbm, lengths_ref), (dest_hbm, dest_ref)], in_sem)
    tok = per_rank * SPAN
    rows = QH * SPAN
    block = 2 * tok + META

    lane = lax.broadcasted_iota(jnp.int32, (META, HD), 1)
    blocks = [(p, base) for p in pieces for base in range(0, p.shape[0], block)]
    for group in range(ids_vmem.shape[0]):
        found = jnp.zeros((META, HD), jnp.float32)
        for i in range(group * HD, min((group + 1) * HD, len(blocks))):
            piece, base = blocks[i]
            meta = piece[base + 2 * tok : base + block, :].astype(jnp.float32)
            found = jnp.where(lane == i - group * HD, meta, found)
        ids_vmem[group] = found.astype(jnp.int32)
    fetch = pltpu.make_async_copy(ids_vmem, ids_smem, id_sem)
    fetch.start()

    for i, (piece, base) in enumerate(blocks):
        kv[2 * tok * i : 2 * tok * (i + 1), :] = piece[base : base + 2 * tok, :]
    for copy in ints:
        copy.wait()
    own_ids = [ids_ref[s] for s in range(per_rank)]
    starts = [history(span, lengths_ref) for span in own_ids]
    first_page = lax.axis_index("seq") * per_rank
    fetch.wait()

    def note(i, found):
        found = list(found)
        for j in range(per_rank):
            number = ids_smem[i // HD, j, i % HD]
            place = (2 * i * per_rank + j) * SPAN
            for s in range(per_rank):
                where[s, found[s]] = place
                seen = (number >= starts[s]) & (number < own_ids[s])
                found[s] = found[s] + seen.astype(jnp.int32)
            to = dest_ref[number] - first_page
            for p in range(per_rank):
                found[per_rank + p] = jnp.where(to == p, place, found[per_rank + p])
        return tuple(found)

    found = (jnp.int32(0),) * per_rank + (jnp.int32(-1),) * per_rank
    found = lax.fori_loop(0, len(blocks), note, found, unroll=len(blocks) <= 16)

    def tile(place):
        return kv[pl.ds(pl.multiple_of(place, SPAN), SPAN), :]

    def page_copy(p):
        return pltpu.make_async_copy(page.at[p], pages_ref.at[p], page_sem.at[p])

    for p in range(per_rank):

        @pl.when(found[per_rank + p] >= 0)
        def _():
            page[p, :, :HD] = tile(found[per_rank + p])
            page[p, :, HD:] = tile(found[per_rank + p] + tok)
            page_copy(p).start()

    def step(at, size, *slots):
        for s in slots:
            places = [where[s, at[s] + i] for i in range(size)]
            keys = jnp.concatenate([tile(p) for p in places], axis=0)
            values = jnp.concatenate([tile(p + tok) for p in places], axis=0)
            own = slice(s * rows, (s + 1) * rows)
            scores = scores_of(q_rot[own, :], keys)
            old = best[own, :]
            top = jnp.maximum(old, jnp.max(scores, axis=1, keepdims=True))
            factor = jnp.exp2((old - top) * SCALE)
            weights = jnp.exp2((scores - jnp.tile(top, (1, size))) * SCALE)
            best[own, :] = top
            total[own, :] = total[own, :] * factor + lanes(weights, jnp.add)
            accum[own, :] = accum[own, :] * factor + jnp.dot(
                weights.astype(jnp.bfloat16), values, preferred_element_type=jnp.float32
            )

    def write(s):
        own = slice(s * SPAN, (s + 1) * SPAN)
        for h in range(QH):
            part = slice(s * rows + h * SPAN, s * rows + (h + 1) * SPAN)
            rows_out[own, h * HD : (h + 1) * HD] = (
                accum[part, :] / jnp.sum(total[part, :], axis=1, keepdims=True)
            ).astype(jnp.bfloat16)
        return pltpu.make_async_copy(rows_out.at[own, :], context_ref.at[own, :], out_sem.at[s])

    seen = found[:per_rank]
    full = [n // LADDER[0] for n in seen]
    shared = functools.reduce(jnp.minimum, full)
    everyone = tuple(range(per_rank))

    @pl.loop(0, shared)
    def _(b):
        step([LADDER[0] * b] * per_rank, LADDER[0], *everyone)

    for s in everyone:

        @pl.loop(shared, full[s])
        def _(b):
            step([LADDER[0] * b] * per_rank, LADDER[0], s)

    for size in LADDER[1:]:
        want = [n % (2 * size) >= size for n in seen]
        at = [n // (2 * size) * (2 * size) for n in seen]
        together = functools.reduce(jnp.logical_and, want)

        @pl.when(together)
        def _():
            step(at, size, *everyone)

        for s in everyone:

            @pl.when(want[s] & jnp.logical_not(together))
            def _():
                step(at, size, s)

    outs = []
    if last:
        for s in everyone:
            outs.append(write(s))
            outs[-1].start()

    for copy in outs:
        copy.wait()
    for p in range(per_rank):

        @pl.when(found[per_rank + p] >= 0)
        def _():
            page_copy(p).wait()


SMEM = pl.BlockSpec(memory_space=pltpu.SMEM)
VMEM = pl.BlockSpec(memory_space=pltpu.VMEM)
ANY = pl.BlockSpec(memory_space=pltpu.HBM)
LIMIT = pltpu.CompilerParams(vmem_limit_bytes=24 << 20)


def vmem(x):
    return pltpu.with_memory_space_constraint(x, pltpu.VMEM)


def hbm(x):
    return pltpu.with_memory_space_constraint(x, pltpu.HBM)


ROUTE = (
    ("A", "o", 8),
    ("B", "o", 4),
    ("X", "o", 2),
    ("co", "o", 1),
    ("BA", "A", 4),
    ("XB", "B", 2),
    ("XA", "A", 2),
    ("cX", "X", 1),
    ("cA", "A", 1),
    ("cB", "B", 1),
    ("XBA", "BA", 2),
    ("cBA", "BA", 1),
    ("cXB", "XB", 1),
    ("cXA", "XA", 1),
    ("cXBA", "XBA", 1),
)
SOON = ("o", "X", "B", "A", "BA", "co", "cX", "cB", "cA", "XB", "cBA")
LATE = ("XA", "cXB", "cXA", "XBA", "cXBA")


def on_device(ranks, queries, keys, values, span_ids, lengths, page_dest):
    return plan(ranks, queries, keys, values, span_ids, lengths, page_dest)


def plan(ranks, queries, keys, values, span_ids, lengths, page_dest):
    tok = queries.shape[0]
    per_rank = span_ids.shape[0]
    spans = page_dest.shape[0]
    block = 2 * tok + META
    rows = per_rank * QH * SPAN
    cosine, sine = (jnp.asarray(t) for t in tables(spans))
    ints = [pltpu.SMEM(x.shape, x.dtype) for x in (span_ids, lengths)]
    turns = [pltpu.VMEM(x.shape, x.dtype) for x in (cosine, sine)]
    packed = pl.pallas_call(
        functools.partial(prepare, spans),
        out_shape=pltpu.VMEM((block, HD), jnp.bfloat16),
        in_specs=[ANY] * 6,
        out_specs=VMEM,
        scratch_shapes=ints
        + [pltpu.VMEM(x.shape, x.dtype) for x in (keys, values)]
        + turns
        + [pltpu.SemaphoreType.DMA((6,))],
        compiler_params=LIMIT,
        name="prepare",
    )(*map(hbm, (span_ids, lengths, keys, values, cosine, sine)))

    def swap(x, distance):
        return lax.ppermute(x, "seq", [(i, i ^ distance) for i in range(ranks)])

    own = packed
    distance = ranks // 2
    while distance >= 16:
        own = jnp.concatenate([own, swap(own, distance)], axis=0)
        distance //= 2
    held = {"o": own}
    for name, source, distance in ROUTE:
        held[name] = swap(held[source], distance)

    state_shapes = tuple(pltpu.VMEM((rows, n), jnp.float32) for n in (HD, HD, HD))
    q_rot, *state = pl.pallas_call(
        functools.partial(early, spans),
        out_shape=(pltpu.VMEM((rows, HD), jnp.bfloat16), *state_shapes),
        in_specs=[ANY] * 5 + [VMEM],
        out_specs=(VMEM,) * 4,
        scratch_shapes=ints
        + [pltpu.VMEM(queries.shape, queries.dtype)]
        + turns
        + [pltpu.SemaphoreType.DMA((5,))],
        compiler_params=LIMIT,
        name="early",
    )(*map(hbm, (span_ids, lengths, queries, cosine, sine)), vmem(packed))

    pages_shape = jax.ShapeDtypeStruct((per_rank, SPAN, 2 * HD), jnp.bfloat16)

    def take(names, last, state, pages):
        pieces = [vmem(held[n]) for n in names]
        length = sum(p.shape[0] for p in pieces)
        units = length // block
        lane_groups = -(-units // HD)
        scratch = [
            pltpu.VMEM((units * 2 * tok, HD), jnp.bfloat16),
            pltpu.VMEM((per_rank, SPAN, 2 * HD), jnp.bfloat16),
            pltpu.VMEM((lane_groups, META, HD), jnp.int32),
            pltpu.SMEM((per_rank, units * per_rank + 4), jnp.int32),
            pltpu.SMEM((lane_groups, META, HD), jnp.int32),
            *[pltpu.SMEM(x.shape, x.dtype) for x in (span_ids, lengths, page_dest)],
            pltpu.SemaphoreType.DMA((3,)),
            pltpu.SemaphoreType.DMA,
            pltpu.SemaphoreType.DMA((per_rank,)),
            pltpu.SemaphoreType.DMA((per_rank,)),
        ]
        if last:
            context_shape = jax.ShapeDtypeStruct((tok, QH * HD), jnp.bfloat16)
            out_shape = (*state_shapes, context_shape, pages_shape)
            out_specs = (VMEM,) * 3 + (ANY, ANY)
            scratch = [pltpu.VMEM((tok, QH * HD), jnp.bfloat16)] + scratch
        else:
            out_shape = (*state_shapes, pages_shape)
            out_specs = (VMEM,) * 3 + (ANY,)
        inputs = [*map(hbm, (span_ids, lengths, page_dest)), vmem(q_rot), *map(vmem, state), *pieces]
        in_specs = [ANY] * 3 + [VMEM] * (4 + len(pieces))
        aliases = {4: 0, 5: 1, 6: 2}
        if last:
            aliases[len(inputs)] = 4
            inputs.append(pages)
            in_specs.append(ANY)
        return pl.pallas_call(
            functools.partial(absorb, per_rank, len(pieces), last),
            out_shape=out_shape,
            in_specs=in_specs,
            out_specs=out_specs,
            scratch_shapes=scratch,
            input_output_aliases=aliases,
            compiler_params=LIMIT,
            name="late" if last else "soon",
        )(*inputs)

    *state, pages = take(SOON, False, state, None)
    *_, context, pages = take(LATE, True, state, pages)
    return context, pages


def solution(mesh):
    return jax.shard_map(
        functools.partial(on_device, mesh.shape["seq"]),
        mesh=mesh,
        in_specs=(
            P(("groups", "seq"), None),
            P(("groups", "seq"), None),
            P(("groups", "seq"), None),
            P(("groups", "seq")),
            P("groups"),
            P("groups"),
        ),
        out_specs=(P(("groups", "seq"), None), P(("groups", "seq"), None, None)),
        check_vma=False,
    )
```

```python
import functools
import math

import jax
import jax.numpy as jnp
import numpy as np
from jax import lax
from jax.experimental import pallas as pl
from jax.experimental.pallas import tpu as pltpu
from jax.sharding import PartitionSpec as P


HD = 128
QH = 6
SPAN = 128
THETA = 1000000.0
NEG = -1e30
META = 8
SCALE = math.log2(math.e) / math.sqrt(HD)


def tables(spans):
    half = HD // 2
    freq = THETA ** (-(np.arange(half, dtype=np.float64) * 2.0 / HD))
    at = np.concatenate([SPAN * np.arange(spans), np.arange(SPAN)]).astype(np.float64)
    angle = at[:, None] * freq[None, :]
    cosine, sine = np.cos(angle), np.sin(angle)
    return (
        np.concatenate([cosine, cosine], axis=1).astype(np.float32),
        np.concatenate([-sine, sine], axis=1).astype(np.float32),
    )


def history(span, lengths_ref):
    start = jnp.int32(0)
    end = jnp.int32(0)
    for i in range(lengths_ref.shape[0]):
        end = end + lengths_ref[i]
        start = jnp.where(end <= span, end, start)
    return start


def turn(cos_ref, sin_ref, spans, depth):
    cos_a, sin_a = cos_ref[pl.ds(depth, 1), :], sin_ref[pl.ds(depth, 1), :]
    cos_b, sin_b = cos_ref[spans : spans + SPAN, :], sin_ref[spans : spans + SPAN, :]
    return cos_a * cos_b - sin_a * sin_b, sin_a * cos_b + cos_a * sin_b


def rotary(x, cosine, sine):
    x = x.astype(jnp.float32)
    return (x * cosine + pltpu.roll(x, HD // 2, 1) * sine).astype(jnp.bfloat16)


def fetch_all(pairs, sems):
    copies = [pltpu.make_async_copy(a, b, sems.at[i]) for i, (a, b) in enumerate(pairs)]
    for copy in copies:
        copy.start()
    return copies


def prepare(spans, *refs):
    out_ref = refs[6]
    ids_ref, lengths_ref, keys_ref, values_ref, cos_ref, sin_ref, sems = refs[7:]
    for copy in fetch_all(list(zip(refs[:6], refs[7:13])), sems):
        copy.wait()
    rows = keys_ref.shape[0]
    row = lax.broadcasted_iota(jnp.int32, (META, HD), 0)
    meta = jnp.zeros((META, HD), jnp.float32)
    for i in range(rows // SPAN):
        span = ids_ref[i]
        cosine, sine = turn(cos_ref, sin_ref, spans, span - history(span, lengths_ref))
        own = slice(i * SPAN, (i + 1) * SPAN)
        out_ref[own, :] = rotary(keys_ref[own, :], cosine, sine)
        meta = jnp.where(row == i, span.astype(jnp.float32), meta)
    out_ref[rows : 2 * rows, :] = values_ref[...]
    out_ref[2 * rows :, :] = meta.astype(jnp.bfloat16)


LADDER = (4, 2, 1)


def lanes(x, combine):
    parts = [x[:, i : i + HD] for i in range(0, x.shape[1], HD)]
    while len(parts) > 1:
        parts = [combine(*parts[i : i + 2]) if i + 1 < len(parts) else parts[i] for i in range(0, len(parts), 2)]
    return parts[0]


def scores_of(queries, keys):
    return lax.dot_general(
        queries, keys, (((1,), (1,)), ((), ())), preferred_element_type=jnp.float32
    )


def attend(queries, keys, values, old, old_total, old_accum, mask=None):
    scores = lax.dot_general(
        queries, keys, (((1,), (1,)), ((), ())), preferred_element_type=jnp.float32
    )
    if mask is not None:
        scores = jnp.where(mask, scores, NEG)
    top = jnp.max(lanes(scores, jnp.maximum), axis=1, keepdims=True)
    top = jnp.broadcast_to(top, (queries.shape[0], HD))
    if old is not None:
        top = jnp.maximum(old, top)
    weights = jnp.exp2((scores - jnp.tile(top, (1, keys.shape[0] // HD))) * SCALE)
    total = lanes(weights, jnp.add)
    accum = jnp.dot(weights.astype(jnp.bfloat16), values, preferred_element_type=jnp.float32)
    if old is not None:
        factor = jnp.exp2((old - top) * SCALE)
        total = total + old_total * factor
        accum = accum + old_accum * factor
    return top, total, accum


def early(spans, *refs):
    own_ref = refs[6]
    info, q_rot, best, total, accum = refs[7:12]
    ids_ref, lengths_ref, dest_ref, queries_ref, cos_ref, sin_ref, sems = refs[12:]
    for copy in fetch_all(list(zip(refs[:6], refs[12:18])), sems):
        copy.wait()
    tok = queries_ref.shape[0]
    per_rank = tok // SPAN
    first_page = lax.axis_index("seq") * per_rank
    for p in range(per_rank):

        def sender(j, span):
            return jnp.where(dest_ref[j] == first_page + p, j, span)

        span = lax.fori_loop(0, spans, sender, jnp.int32(0), unroll=8)
        info[2 * per_rank + p : 2 * per_rank + p + 1, :] = jnp.full((1, HD), span, jnp.int32)
    rows = QH * SPAN
    row = lax.broadcasted_iota(jnp.int32, (rows, SPAN), 0) % SPAN
    key = lax.broadcasted_iota(jnp.int32, (rows, SPAN), 1)
    causal = key <= row
    for s in range(tok // SPAN):
        span = ids_ref[s]
        start = history(span, lengths_ref)
        info[s : s + 1, :] = jnp.full((1, HD), start, jnp.int32)
        info[per_rank + s : per_rank + s + 1, :] = jnp.full((1, HD), span, jnp.int32)
        cosine, sine = turn(cos_ref, sin_ref, spans, span - start)
        for h in range(QH):
            q_rot[s * rows + h * SPAN : s * rows + (h + 1) * SPAN, :] = rotary(
                queries_ref[s * SPAN : (s + 1) * SPAN, h * HD : (h + 1) * HD], cosine, sine
            )
        keys = own_ref[s * SPAN : (s + 1) * SPAN, :]
        values = own_ref[tok + s * SPAN : tok + (s + 1) * SPAN, :]
        own = slice(s * rows, (s + 1) * rows)
        best[own, :], total[own, :], accum[own, :] = attend(
            q_rot[own, :], keys, values, None, None, None, causal
        )


def absorb(
    per_rank, count, last, info, q_rot, best_in, total_in, accum_in, *rest
):
    pieces, rest = rest[:count], rest[count:]
    if last:
        _, best, total, accum, context_ref, pages_ref, rows_out = rest[:7]
        rest = rest[7:]
    else:
        best, total, accum, pages_ref = rest[:4]
        rest = rest[4:]
    kv, page, where, page_sem, out_sem = rest
    tok = per_rank * SPAN
    rows = QH * SPAN
    block = 2 * tok + META

    blocks = [(p, base) for p in pieces for base in range(0, p.shape[0], block)]
    lane = lax.broadcasted_iota(jnp.int32, (META, HD), 1)
    slot = lax.broadcasted_iota(jnp.int32, (META, HD), 0)
    found = [jnp.int32(0)] * per_rank
    pages = [jnp.int32(0)] * per_rank
    group = 24 // per_rank
    for first in range(0, len(blocks), group):
        some = blocks[first : first + group]
        numbers = jnp.full((META, HD), -1.0, jnp.float32)
        for i, (piece, base) in enumerate(some):
            meta = piece[base + 2 * tok : base + block, :].astype(jnp.float32)
            numbers = jnp.where(lane == i, meta, numbers)
        numbers = numbers.astype(jnp.int32)
        valid = (slot < per_rank) & (lane < len(some))
        weight = jnp.left_shift(1, jnp.where(valid, lane * per_rank + slot, 0)).astype(jnp.float32)
        places = ((2 * (first + lane) * per_rank + slot) * SPAN + 1).astype(jnp.float32)

        def row(i):
            return info[i : i + 1, :]

        def choose(mask, x):
            return jnp.sum(jnp.where(mask & valid, x, 0.0)).astype(jnp.int32)

        bits = [choose((numbers >= row(s)) & (numbers < row(per_rank + s)), weight) for s in range(per_rank)]
        for p in range(per_rank):
            pages[p] = pages[p] + choose(numbers == row(2 * per_rank + p), places)
        for i in range(len(some)):
            for j in range(per_rank):
                for s in range(per_rank):
                    where[s, found[s]] = (2 * (first + i) * per_rank + j) * SPAN
                    found[s] = found[s] + (jnp.right_shift(bits[s], i * per_rank + j) & 1)

    for i, (piece, base) in enumerate(blocks):
        kv[2 * tok * i : 2 * tok * (i + 1), :] = piece[base : base + 2 * tok, :]

    def tile(place):
        return kv[pl.ds(pl.multiple_of(place, SPAN), SPAN), :]

    def page_copy(p):
        return pltpu.make_async_copy(page.at[p], pages_ref.at[p], page_sem.at[p])

    for p in range(per_rank):

        @pl.when(pages[p] > 0)
        def _():
            page[p, :, :HD] = tile(pages[p] - 1)
            page[p, :, HD:] = tile(pages[p] - 1 + tok)
            page_copy(p).start()

    def step(at, size, *slots):
        for s in slots:
            places = [where[s, at[s] + i] for i in range(size)]
            keys = jnp.concatenate([tile(p) for p in places], axis=0)
            values = jnp.concatenate([tile(p + tok) for p in places], axis=0)
            own = slice(s * rows, (s + 1) * rows)
            scores = scores_of(q_rot[own, :], keys)
            old = best[own, :]
            top = jnp.maximum(old, jnp.max(scores, axis=1, keepdims=True))
            factor = jnp.exp2((old - top) * SCALE)
            weights = jnp.exp2((scores - jnp.tile(top, (1, size))) * SCALE)
            best[own, :] = top
            total[own, :] = total[own, :] * factor + lanes(weights, jnp.add)
            accum[own, :] = accum[own, :] * factor + jnp.dot(
                weights.astype(jnp.bfloat16), values, preferred_element_type=jnp.float32
            )

    def write(s):
        own = slice(s * SPAN, (s + 1) * SPAN)
        for h in range(QH):
            part = slice(s * rows + h * SPAN, s * rows + (h + 1) * SPAN)
            rows_out[own, h * HD : (h + 1) * HD] = (
                accum[part, :] / jnp.sum(total[part, :], axis=1, keepdims=True)
            ).astype(jnp.bfloat16)
        return pltpu.make_async_copy(rows_out.at[own, :], context_ref.at[own, :], out_sem.at[s])

    seen = found
    full = [n // LADDER[0] for n in seen]
    shared = functools.reduce(jnp.minimum, full)
    everyone = tuple(range(per_rank))

    @pl.loop(0, shared)
    def _(b):
        step([LADDER[0] * b] * per_rank, LADDER[0], *everyone)

    for s in everyone:

        @pl.loop(shared, full[s])
        def _(b):
            step([LADDER[0] * b] * per_rank, LADDER[0], s)

    for size in LADDER[1:]:
        want = [n % (2 * size) >= size for n in seen]
        at = [n // (2 * size) * (2 * size) for n in seen]
        together = functools.reduce(jnp.logical_and, want)

        @pl.when(together)
        def _():
            step(at, size, *everyone)

        for s in everyone:

            @pl.when(want[s] & jnp.logical_not(together))
            def _():
                step(at, size, s)

    outs = []
    if last:
        for s in everyone:
            outs.append(write(s))
            outs[-1].start()

    for copy in outs:
        copy.wait()
    for p in range(per_rank):

        @pl.when(pages[p] > 0)
        def _():
            page_copy(p).wait()


SMEM = pl.BlockSpec(memory_space=pltpu.SMEM)
VMEM = pl.BlockSpec(memory_space=pltpu.VMEM)
ANY = pl.BlockSpec(memory_space=pltpu.HBM)
LIMIT = pltpu.CompilerParams(vmem_limit_bytes=24 << 20)


def vmem(x):
    return pltpu.with_memory_space_constraint(x, pltpu.VMEM)


def hbm(x):
    return pltpu.with_memory_space_constraint(x, pltpu.HBM)


ROUTE = (
    ("A", "o", 8),
    ("B", "o", 4),
    ("X", "o", 2),
    ("co", "o", 1),
    ("BA", "A", 4),
    ("XB", "B", 2),
    ("XA", "A", 2),
    ("cX", "X", 1),
    ("cA", "A", 1),
    ("cB", "B", 1),
    ("XBA", "BA", 2),
    ("cBA", "BA", 1),
    ("cXB", "XB", 1),
    ("cXA", "XA", 1),
    ("cXBA", "XBA", 1),
)
SOON = ("o", "X", "B", "A", "BA", "co", "cX", "cB", "cA", "XB", "cBA")
LATE = ("XA", "cXB", "cXA", "XBA", "cXBA")


def on_device(ranks, queries, keys, values, span_ids, lengths, page_dest):
    return plan(ranks, queries, keys, values, span_ids, lengths, page_dest)


def plan(ranks, queries, keys, values, span_ids, lengths, page_dest):
    tok = queries.shape[0]
    per_rank = span_ids.shape[0]
    spans = page_dest.shape[0]
    block = 2 * tok + META
    rows = per_rank * QH * SPAN
    cosine, sine = (jnp.asarray(t) for t in tables(spans))
    ints = [pltpu.SMEM(x.shape, x.dtype) for x in (span_ids, lengths)]
    turns = [pltpu.VMEM(x.shape, x.dtype) for x in (cosine, sine)]
    packed = pl.pallas_call(
        functools.partial(prepare, spans),
        out_shape=pltpu.VMEM((block, HD), jnp.bfloat16),
        in_specs=[ANY] * 6,
        out_specs=VMEM,
        scratch_shapes=ints
        + [pltpu.VMEM(x.shape, x.dtype) for x in (keys, values)]
        + turns
        + [pltpu.SemaphoreType.DMA((6,))],
        compiler_params=LIMIT,
        name="prepare",
    )(*map(hbm, (span_ids, lengths, keys, values, cosine, sine)))

    def swap(x, distance):
        return lax.ppermute(x, "seq", [(i, i ^ distance) for i in range(ranks)])

    own = packed
    distance = ranks // 2
    while distance >= 16:
        own = jnp.concatenate([own, swap(own, distance)], axis=0)
        distance //= 2
    held = {"o": own}
    for name, source, distance in ROUTE:
        held[name] = swap(held[source], distance)

    state_shapes = tuple(pltpu.VMEM((rows, n), jnp.float32) for n in (HD, HD, HD))
    info, q_rot, *state = pl.pallas_call(
        functools.partial(early, spans),
        out_shape=(
            pltpu.VMEM((-(-3 * per_rank // 8) * 8, HD), jnp.int32),
            pltpu.VMEM((rows, HD), jnp.bfloat16),
            *state_shapes,
        ),
        in_specs=[ANY] * 6 + [VMEM],
        out_specs=(VMEM,) * 5,
        scratch_shapes=ints
        + [pltpu.SMEM(page_dest.shape, page_dest.dtype), pltpu.VMEM(queries.shape, queries.dtype)]
        + turns
        + [pltpu.SemaphoreType.DMA((6,))],
        compiler_params=LIMIT,
        name="early",
    )(*map(hbm, (span_ids, lengths, page_dest, queries, cosine, sine)), vmem(packed))

    pages_shape = jax.ShapeDtypeStruct((per_rank, SPAN, 2 * HD), jnp.bfloat16)

    def take(names, last, state, pages):
        pieces = [vmem(held[n]) for n in names]
        length = sum(p.shape[0] for p in pieces)
        units = length // block
        scratch = [
            pltpu.VMEM((units * 2 * tok, HD), jnp.bfloat16),
            pltpu.VMEM((per_rank, SPAN, 2 * HD), jnp.bfloat16),
            pltpu.SMEM((per_rank, units * per_rank + 4), jnp.int32),
            pltpu.SemaphoreType.DMA((per_rank,)),
            pltpu.SemaphoreType.DMA((per_rank,)),
        ]
        if last:
            context_shape = jax.ShapeDtypeStruct((tok, QH * HD), jnp.bfloat16)
            out_shape = (*state_shapes, context_shape, pages_shape)
            out_specs = (VMEM,) * 3 + (ANY, ANY)
            scratch = [pltpu.VMEM((tok, QH * HD), jnp.bfloat16)] + scratch
        else:
            out_shape = (*state_shapes, pages_shape)
            out_specs = (VMEM,) * 3 + (ANY,)
        inputs = [vmem(info), vmem(q_rot), *map(vmem, state), *pieces]
        in_specs = [VMEM] * (5 + len(pieces))
        aliases = {2: 0, 3: 1, 4: 2}
        if last:
            aliases[len(inputs)] = 4
            inputs.append(pages)
            in_specs.append(ANY)
        return pl.pallas_call(
            functools.partial(absorb, per_rank, len(pieces), last),
            out_shape=out_shape,
            in_specs=in_specs,
            out_specs=out_specs,
            scratch_shapes=scratch,
            input_output_aliases=aliases,
            compiler_params=LIMIT,
            name="late" if last else "soon",
        )(*inputs)

    *state, pages = take(SOON, False, state, None)
    *_, context, pages = take(LATE, True, state, pages)
    return context, pages


def solution(mesh):
    return jax.shard_map(
        functools.partial(on_device, mesh.shape["seq"]),
        mesh=mesh,
        in_specs=(
            P(("groups", "seq"), None),
            P(("groups", "seq"), None),
            P(("groups", "seq"), None),
            P(("groups", "seq")),
            P("groups"),
            P("groups"),
        ),
        out_specs=(P(("groups", "seq"), None), P(("groups", "seq"), None, None)),
        check_vma=False,
    )
```

```python
import functools
import math

import jax
import jax.numpy as jnp
import numpy as np
from jax import lax
from jax.experimental import pallas as pl
from jax.experimental.pallas import tpu as pltpu
from jax.sharding import PartitionSpec as P


HD = 128
QH = 6
SPAN = 128
THETA = 1000000.0
NEG = -1e30
META = 8
SCALE = math.log2(math.e) / math.sqrt(HD)


def tables(spans):
    half = HD // 2
    freq = THETA ** (-(np.arange(half, dtype=np.float64) * 2.0 / HD))
    at = np.concatenate([SPAN * np.arange(spans), np.arange(SPAN)]).astype(np.float64)
    angle = at[:, None] * freq[None, :]
    cosine, sine = np.cos(angle), np.sin(angle)
    return (
        np.concatenate([cosine, cosine], axis=1).astype(np.float32),
        np.concatenate([-sine, sine], axis=1).astype(np.float32),
    )


def history(span, lengths_ref):
    start = jnp.int32(0)
    end = jnp.int32(0)
    for i in range(lengths_ref.shape[0]):
        end = end + lengths_ref[i]
        start = jnp.where(end <= span, end, start)
    return start


def turn(cos_ref, sin_ref, spans, depth):
    cos_a, sin_a = cos_ref[pl.ds(depth, 1), :], sin_ref[pl.ds(depth, 1), :]
    cos_b, sin_b = cos_ref[spans : spans + SPAN, :], sin_ref[spans : spans + SPAN, :]
    return cos_a * cos_b - sin_a * sin_b, sin_a * cos_b + cos_a * sin_b


def rotary(x, cosine, sine):
    x = x.astype(jnp.float32)
    return (x * cosine + pltpu.roll(x, HD // 2, 1) * sine).astype(jnp.bfloat16)


def fetch_all(pairs, sems):
    copies = [pltpu.make_async_copy(a, b, sems.at[i]) for i, (a, b) in enumerate(pairs)]
    for copy in copies:
        copy.start()
    return copies


def prepare(spans, *refs):
    out_ref = refs[6]
    ids_ref, lengths_ref, keys_ref, values_ref, cos_ref, sin_ref, sems = refs[7:]
    for copy in fetch_all(list(zip(refs[:6], refs[7:13])), sems):
        copy.wait()
    rows = keys_ref.shape[0]
    row = lax.broadcasted_iota(jnp.int32, (META, HD), 0)
    meta = jnp.zeros((META, HD), jnp.float32)
    for i in range(rows // SPAN):
        span = ids_ref[i]
        cosine, sine = turn(cos_ref, sin_ref, spans, span - history(span, lengths_ref))
        own = slice(i * SPAN, (i + 1) * SPAN)
        out_ref[own, :] = rotary(keys_ref[own, :], cosine, sine)
        meta = jnp.where(row == i, span.astype(jnp.float32), meta)
    out_ref[rows : 2 * rows, :] = values_ref[...]
    out_ref[2 * rows :, :] = meta.astype(jnp.bfloat16)


LADDER = 4


def lanes(x, combine):
    parts = [x[:, i : i + HD] for i in range(0, x.shape[1], HD)]
    while len(parts) > 1:
        parts = [combine(*parts[i : i + 2]) if i + 1 < len(parts) else parts[i] for i in range(0, len(parts), 2)]
    return parts[0]


def scores_of(queries, keys):
    return lax.dot_general(
        queries, keys, (((1,), (1,)), ((), ())), preferred_element_type=jnp.float32
    )


def attend(queries, keys, values, old, old_total, old_accum, mask=None):
    scores = lax.dot_general(
        queries, keys, (((1,), (1,)), ((), ())), preferred_element_type=jnp.float32
    )
    if mask is not None:
        scores = jnp.where(mask, scores, NEG)
    top = jnp.max(lanes(scores, jnp.maximum), axis=1, keepdims=True)
    top = jnp.broadcast_to(top, (queries.shape[0], HD))
    if old is not None:
        top = jnp.maximum(old, top)
    weights = jnp.exp2((scores - jnp.tile(top, (1, keys.shape[0] // HD))) * SCALE)
    total = lanes(weights, jnp.add)
    accum = jnp.dot(weights.astype(jnp.bfloat16), values, preferred_element_type=jnp.float32)
    if old is not None:
        factor = jnp.exp2((old - top) * SCALE)
        total = total + old_total * factor
        accum = accum + old_accum * factor
    return top, total, accum


def early(spans, *refs):
    own_ref = refs[6]
    info, q_rot, best, total, accum = refs[7:12]
    ids_ref, lengths_ref, dest_ref, queries_ref, cos_ref, sin_ref, sems = refs[12:]
    for copy in fetch_all(list(zip(refs[:6], refs[12:18])), sems):
        copy.wait()
    tok = queries_ref.shape[0]
    per_rank = tok // SPAN
    first_page = lax.axis_index("seq") * per_rank
    for p in range(per_rank):

        def sender(j, span):
            return jnp.where(dest_ref[j] == first_page + p, j, span)

        span = lax.fori_loop(0, spans, sender, jnp.int32(0), unroll=8)
        info[2 * per_rank + p : 2 * per_rank + p + 1, :] = jnp.full((1, HD), span, jnp.int32)
    rows = QH * SPAN
    row = lax.broadcasted_iota(jnp.int32, (rows, SPAN), 0) % SPAN
    key = lax.broadcasted_iota(jnp.int32, (rows, SPAN), 1)
    causal = key <= row
    for s in range(tok // SPAN):
        span = ids_ref[s]
        start = history(span, lengths_ref)
        info[s : s + 1, :] = jnp.full((1, HD), start, jnp.int32)
        info[per_rank + s : per_rank + s + 1, :] = jnp.full((1, HD), span, jnp.int32)
        cosine, sine = turn(cos_ref, sin_ref, spans, span - start)
        for h in range(QH):
            q_rot[s * rows + h * SPAN : s * rows + (h + 1) * SPAN, :] = rotary(
                queries_ref[s * SPAN : (s + 1) * SPAN, h * HD : (h + 1) * HD], cosine, sine
            )
        keys = own_ref[s * SPAN : (s + 1) * SPAN, :]
        values = own_ref[tok + s * SPAN : tok + (s + 1) * SPAN, :]
        own = slice(s * rows, (s + 1) * rows)
        best[own, :], total[own, :], accum[own, :] = attend(
            q_rot[own, :], keys, values, None, None, None, causal
        )


def absorb(
    per_rank, count, fresh, last, info, q_rot, best_in, total_in, accum_in, *rest
):
    pieces, rest = rest[:count], rest[count:]
    rest = rest[0 if fresh else 1 :]
    if last:
        best, total, accum, context_ref, pages_ref, rows_out = rest[:6]
        rest = rest[6:]
    else:
        best, total, accum, pages_ref = rest[:4]
        rest = rest[4:]
    kv, page, where, page_sem, out_sem = rest
    tok = per_rank * SPAN
    rows = QH * SPAN
    block = 2 * tok + META

    blocks = [(p, base) for p in pieces for base in range(0, p.shape[0], block)]
    lane = lax.broadcasted_iota(jnp.int32, (META, HD), 1)
    slot = lax.broadcasted_iota(jnp.int32, (META, HD), 0)
    found = [jnp.int32(0)] * per_rank
    pages = [jnp.int32(0)] * per_rank
    group = 24 // per_rank
    for first in range(0, len(blocks), group):
        some = blocks[first : first + group]
        numbers = jnp.full((META, HD), -1.0, jnp.float32)
        for i, (piece, base) in enumerate(some):
            meta = piece[base + 2 * tok : base + block, :].astype(jnp.float32)
            numbers = jnp.where(lane == i, meta, numbers)
        numbers = numbers.astype(jnp.int32)
        valid = (slot < per_rank) & (lane < len(some))
        weight = jnp.left_shift(1, jnp.where(valid, lane * per_rank + slot, 0)).astype(jnp.float32)
        places = ((2 * (first + lane) * per_rank + slot) * SPAN + 1).astype(jnp.float32)

        def row(i):
            return info[i : i + 1, :]

        def choose(mask, x):
            return jnp.sum(jnp.where(mask & valid, x, 0.0)).astype(jnp.int32)

        bits = [choose((numbers >= row(s)) & (numbers < row(per_rank + s)), weight) for s in range(per_rank)]
        for p in range(per_rank):
            pages[p] = pages[p] + choose(numbers == row(2 * per_rank + p), places)
        for i in range(len(some)):
            for j in range(per_rank):
                for s in range(per_rank):
                    where[s, found[s]] = (2 * (first + i) * per_rank + j) * SPAN
                    found[s] = found[s] + (jnp.right_shift(bits[s], i * per_rank + j) & 1)

    for i, (piece, base) in enumerate(blocks):
        kv[2 * tok * i : 2 * tok * (i + 1), :] = piece[base : base + 2 * tok, :]

    def tile(place):
        return kv[pl.ds(pl.multiple_of(place, SPAN), SPAN), :]

    def page_copy(p):
        return pltpu.make_async_copy(page.at[p], pages_ref.at[p], page_sem.at[p])

    for p in range(per_rank):

        @pl.when(pages[p] > 0)
        def _():
            page[p, :, :HD] = tile(pages[p] - 1)
            page[p, :, HD:] = tile(pages[p] - 1 + tok)
            page_copy(p).start()

    def step(at, size, *slots):
        places = [[where[s, at[s] + i] for i in range(size)] for s in slots]
        own = slice(slots[0] * rows, (slots[-1] + 1) * rows)
        scores = jnp.concatenate(
            [
                scores_of(q_rot[s * rows : (s + 1) * rows, :], jnp.concatenate([tile(p) for p in some], axis=0))
                for s, some in zip(slots, places)
            ],
            axis=0,
        )
        old = best[own, :]
        top = jnp.maximum(old, jnp.max(scores, axis=1, keepdims=True))
        factor = jnp.exp2((old - top) * SCALE)
        weights = jnp.exp2((scores - jnp.tile(top, (1, size))) * SCALE)
        best[own, :] = top
        total[own, :] = total[own, :] * factor + lanes(weights, jnp.add)
        weights = weights.astype(jnp.bfloat16)
        accum[own, :] = accum[own, :] * factor + jnp.concatenate(
            [
                jnp.dot(
                    weights[i * rows : (i + 1) * rows, :],
                    jnp.concatenate([tile(p + tok) for p in some], axis=0),
                    preferred_element_type=jnp.float32,
                )
                for i, some in enumerate(places)
            ],
            axis=0,
        )

    def write(s):
        own = slice(s * SPAN, (s + 1) * SPAN)
        for h in range(QH):
            part = slice(s * rows + h * SPAN, s * rows + (h + 1) * SPAN)
            rows_out[own, h * HD : (h + 1) * HD] = (
                accum[part, :] / jnp.sum(total[part, :], axis=1, keepdims=True)
            ).astype(jnp.bfloat16)
        return pltpu.make_async_copy(rows_out.at[own, :], context_ref.at[own, :], out_sem.at[s])

    seen = found
    full = [n // LADDER for n in seen]
    shared = functools.reduce(jnp.minimum, full)
    everyone = tuple(range(per_rank))

    @pl.loop(0, shared)
    def _(b):
        step([LADDER * b] * per_rank, LADDER, *everyone)

    for s in everyone:

        @pl.loop(shared, full[s])
        def _(b):
            step([LADDER * b] * per_rank, LADDER, s)

    at = [LADDER * n for n in full]
    for size in range(LADDER - 1, 0, -1):
        want = [n % LADDER == size for n in seen]
        together = functools.reduce(jnp.logical_and, want)

        @pl.when(together)
        def _():
            step(at, size, *everyone)

        for s in everyone:

            @pl.when(want[s] & jnp.logical_not(together))
            def _():
                step(at, size, s)

    outs = []
    if last:
        for s in everyone:
            outs.append(write(s))
            outs[-1].start()

    for copy in outs:
        copy.wait()
    for p in range(per_rank):

        @pl.when(pages[p] > 0)
        def _():
            page_copy(p).wait()


SMEM = pl.BlockSpec(memory_space=pltpu.SMEM)
VMEM = pl.BlockSpec(memory_space=pltpu.VMEM)
ANY = pl.BlockSpec(memory_space=pltpu.HBM)
LIMIT = pltpu.CompilerParams(vmem_limit_bytes=24 << 20)


def vmem(x):
    return pltpu.with_memory_space_constraint(x, pltpu.VMEM)


def hbm(x):
    return pltpu.with_memory_space_constraint(x, pltpu.HBM)


ROUTE = (
    ("v1", "o", 4, 8),
    ("v2", "o", 8, 2),
    ("v3", "o", 2, 4),
    ("co", "o", 1, 1),
    ("v4", "v1", 2, 2),
    ("v5", "v1", 8, 4),
    ("v6", "v2", 2, 4),
    ("cv3", "v3", 1, 1),
    ("cv1", "v1", 1, 1),
    ("cv2", "v2", 1, 1),
    ("v7", "v4", 8, 4),
    ("cv4", "v4", 1, 1),
    ("cv5", "v5", 1, 1),
    ("cv6", "v6", 1, 1),
    ("cv7", "v7", 1, 1),
)
SOON = ("o", "v1", "v2", "v3", "co", "cv1", "cv2", "cv3", "v4", "cv4", "v5")
MID = ("v6", "cv5", "v7")
LATE = ("cv6", "cv7")


def on_device(ranks, queries, keys, values, span_ids, lengths, page_dest):
    return plan(ranks, queries, keys, values, span_ids, lengths, page_dest)


def plan(ranks, queries, keys, values, span_ids, lengths, page_dest):
    tok = queries.shape[0]
    per_rank = span_ids.shape[0]
    spans = page_dest.shape[0]
    block = 2 * tok + META
    rows = per_rank * QH * SPAN
    cosine, sine = (jnp.asarray(t) for t in tables(spans))
    ints = [pltpu.SMEM(x.shape, x.dtype) for x in (span_ids, lengths)]
    turns = [pltpu.VMEM(x.shape, x.dtype) for x in (cosine, sine)]
    packed = pl.pallas_call(
        functools.partial(prepare, spans),
        out_shape=pltpu.VMEM((block, HD), jnp.bfloat16),
        in_specs=[ANY] * 6,
        out_specs=VMEM,
        scratch_shapes=ints
        + [pltpu.VMEM(x.shape, x.dtype) for x in (keys, values)]
        + turns
        + [pltpu.SemaphoreType.DMA((6,))],
        compiler_params=LIMIT,
        name="prepare",
    )(*map(hbm, (span_ids, lengths, keys, values, cosine, sine)))

    def swap(x, even, odd):
        return lax.ppermute(x, "seq", [(i, i ^ (odd if i % 2 else even)) for i in range(ranks)])

    own = packed
    distance = ranks // 2
    while distance >= 16:
        own = jnp.concatenate([own, swap(own, distance, distance)], axis=0)
        distance //= 2
    held = {"o": own}
    for name, source, even, odd in ROUTE:
        held[name] = swap(held[source], even, odd)

    state_shapes = tuple(pltpu.VMEM((rows, n), jnp.float32) for n in (HD, HD, HD))
    info, q_rot, *state = pl.pallas_call(
        functools.partial(early, spans),
        out_shape=(
            pltpu.VMEM((-(-3 * per_rank // 8) * 8, HD), jnp.int32),
            pltpu.VMEM((rows, HD), jnp.bfloat16),
            *state_shapes,
        ),
        in_specs=[ANY] * 6 + [VMEM],
        out_specs=(VMEM,) * 5,
        scratch_shapes=ints
        + [pltpu.SMEM(page_dest.shape, page_dest.dtype), pltpu.VMEM(queries.shape, queries.dtype)]
        + turns
        + [pltpu.SemaphoreType.DMA((6,))],
        compiler_params=LIMIT,
        name="early",
    )(*map(hbm, (span_ids, lengths, page_dest, queries, cosine, sine)), vmem(packed))

    pages_shape = jax.ShapeDtypeStruct((per_rank, SPAN, 2 * HD), jnp.bfloat16)

    def take(names, state, pages, last=False):
        pieces = [vmem(held[n]) for n in names]
        length = sum(p.shape[0] for p in pieces)
        units = length // block
        scratch = [
            pltpu.VMEM((units * 2 * tok, HD), jnp.bfloat16),
            pltpu.VMEM((per_rank, SPAN, 2 * HD), jnp.bfloat16),
            pltpu.SMEM((per_rank, units * per_rank + 4), jnp.int32),
            pltpu.SemaphoreType.DMA((per_rank,)),
            pltpu.SemaphoreType.DMA((per_rank,)),
        ]
        if last:
            context_shape = jax.ShapeDtypeStruct((tok, QH * HD), jnp.bfloat16)
            out_shape = (*state_shapes, context_shape, pages_shape)
            out_specs = (VMEM,) * 3 + (ANY, ANY)
            scratch = [pltpu.VMEM((tok, QH * HD), jnp.bfloat16)] + scratch
        else:
            out_shape = (*state_shapes, pages_shape)
            out_specs = (VMEM,) * 3 + (ANY,)
        inputs = [vmem(info), vmem(q_rot), *map(vmem, state), *pieces]
        in_specs = [VMEM] * (5 + len(pieces))
        aliases = {2: 0, 3: 1, 4: 2}
        if pages is not None:
            aliases[len(inputs)] = len(out_shape) - 1
            inputs.append(pages)
            in_specs.append(ANY)
        return pl.pallas_call(
            functools.partial(absorb, per_rank, len(pieces), pages is None, last),
            out_shape=out_shape,
            in_specs=in_specs,
            out_specs=out_specs,
            scratch_shapes=scratch,
            input_output_aliases=aliases,
            compiler_params=LIMIT,
        )(*inputs)

    *state, pages = take(SOON, state, None)
    *state, pages = take(MID, state, pages)
    *_, context, pages = take(LATE, state, pages, last=True)
    return context, pages


def solution(mesh):
    return jax.shard_map(
        functools.partial(on_device, mesh.shape["seq"]),
        mesh=mesh,
        in_specs=(
            P(("groups", "seq"), None),
            P(("groups", "seq"), None),
            P(("groups", "seq"), None),
            P(("groups", "seq")),
            P("groups"),
            P("groups"),
        ),
        out_specs=(P(("groups", "seq"), None), P(("groups", "seq"), None, None)),
        check_vma=False,
    )
```

```python
import functools
import math

import jax
import jax.numpy as jnp
import numpy as np
from jax import lax
from jax.experimental import pallas as pl
from jax.experimental.pallas import tpu as pltpu
from jax.sharding import PartitionSpec as P


HD = 128
QH = 6
SPAN = 128
THETA = 1000000.0
NEG = -1e30
META = 8
SCALE = math.log2(math.e) / math.sqrt(HD)


def tables(spans):
    half = HD // 2
    freq = THETA ** (-(np.arange(half, dtype=np.float64) * 2.0 / HD))
    at = np.concatenate([SPAN * np.arange(spans), np.arange(SPAN)]).astype(np.float64)
    angle = at[:, None] * freq[None, :]
    cosine, sine = np.cos(angle), np.sin(angle)
    return (
        np.concatenate([cosine, cosine], axis=1).astype(np.float32),
        np.concatenate([-sine, sine], axis=1).astype(np.float32),
    )


def history(span, lengths_ref):
    start = jnp.int32(0)
    end = jnp.int32(0)
    for i in range(lengths_ref.shape[0]):
        end = end + lengths_ref[i]
        start = jnp.where(end <= span, end, start)
    return start


def turn(cos_ref, sin_ref, spans, depth):
    cos_a, sin_a = cos_ref[pl.ds(depth, 1), :], sin_ref[pl.ds(depth, 1), :]
    cos_b, sin_b = cos_ref[spans : spans + SPAN, :], sin_ref[spans : spans + SPAN, :]
    return cos_a * cos_b - sin_a * sin_b, sin_a * cos_b + cos_a * sin_b


def rotary(x, cosine, sine):
    x = x.astype(jnp.float32)
    return (x * cosine + pltpu.roll(x, HD // 2, 1) * sine).astype(jnp.bfloat16)


def fetch_all(pairs, sems):
    copies = [pltpu.make_async_copy(a, b, sems.at[i]) for i, (a, b) in enumerate(pairs)]
    for copy in copies:
        copy.start()
    return copies


def prepare(spans, *refs):
    out_ref = refs[6]
    ids_ref, lengths_ref, keys_ref, values_ref, cos_ref, sin_ref, sems = refs[7:]
    for copy in fetch_all(list(zip(refs[:6], refs[7:13])), sems):
        copy.wait()
    rows = keys_ref.shape[0]
    row = lax.broadcasted_iota(jnp.int32, (META, HD), 0)
    meta = jnp.zeros((META, HD), jnp.float32)
    for i in range(rows // SPAN):
        span = ids_ref[i]
        cosine, sine = turn(cos_ref, sin_ref, spans, span - history(span, lengths_ref))
        own = slice(i * SPAN, (i + 1) * SPAN)
        out_ref[own, :] = rotary(keys_ref[own, :], cosine, sine)
        meta = jnp.where(row == i, span.astype(jnp.float32), meta)
    out_ref[rows : 2 * rows, :] = values_ref[...]
    out_ref[2 * rows :, :] = meta.astype(jnp.bfloat16)


LADDER = 4


def lanes(x, combine):
    parts = [x[:, i : i + HD] for i in range(0, x.shape[1], HD)]
    while len(parts) > 1:
        parts = [combine(*parts[i : i + 2]) if i + 1 < len(parts) else parts[i] for i in range(0, len(parts), 2)]
    return parts[0]


def scores_of(queries, keys):
    return lax.dot_general(
        queries, keys, (((1,), (1,)), ((), ())), preferred_element_type=jnp.float32
    )


def attend(queries, keys, values, old, old_total, old_accum, mask=None):
    scores = lax.dot_general(
        queries, keys, (((1,), (1,)), ((), ())), preferred_element_type=jnp.float32
    )
    if mask is not None:
        scores = jnp.where(mask, scores, NEG)
    top = jnp.max(lanes(scores, jnp.maximum), axis=1, keepdims=True)
    top = jnp.broadcast_to(top, (queries.shape[0], HD))
    if old is not None:
        top = jnp.maximum(old, top)
    weights = jnp.exp2((scores - jnp.tile(top, (1, keys.shape[0] // HD))) * SCALE)
    total = lanes(weights, jnp.add)
    accum = jnp.dot(weights.astype(jnp.bfloat16), values, preferred_element_type=jnp.float32)
    if old is not None:
        factor = jnp.exp2((old - top) * SCALE)
        total = total + old_total * factor
        accum = accum + old_accum * factor
    return top, total, accum


def early(spans, *refs):
    own_ref = refs[6]
    info, q_rot, best, total, accum = refs[7:12]
    ids_ref, lengths_ref, dest_ref, queries_ref, cos_ref, sin_ref, sems = refs[12:]
    for copy in fetch_all(list(zip(refs[:6], refs[12:18])), sems):
        copy.wait()
    tok = queries_ref.shape[0]
    per_rank = tok // SPAN
    first_page = lax.axis_index("seq") * per_rank
    for p in range(per_rank):

        def sender(j, span):
            return jnp.where(dest_ref[j] == first_page + p, j, span)

        span = lax.fori_loop(0, spans, sender, jnp.int32(0), unroll=8)
        info[2 * per_rank + p : 2 * per_rank + p + 1, :] = jnp.full((1, HD), span, jnp.int32)
    rows = QH * SPAN
    row = lax.broadcasted_iota(jnp.int32, (rows, SPAN), 0) % SPAN
    key = lax.broadcasted_iota(jnp.int32, (rows, SPAN), 1)
    causal = key <= row
    for s in range(tok // SPAN):
        span = ids_ref[s]
        start = history(span, lengths_ref)
        info[s : s + 1, :] = jnp.full((1, HD), start, jnp.int32)
        info[per_rank + s : per_rank + s + 1, :] = jnp.full((1, HD), span, jnp.int32)
        cosine, sine = turn(cos_ref, sin_ref, spans, span - start)
        for h in range(QH):
            q_rot[s * rows + h * SPAN : s * rows + (h + 1) * SPAN, :] = rotary(
                queries_ref[s * SPAN : (s + 1) * SPAN, h * HD : (h + 1) * HD], cosine, sine
            )
        keys = own_ref[s * SPAN : (s + 1) * SPAN, :]
        values = own_ref[tok + s * SPAN : tok + (s + 1) * SPAN, :]
        own = slice(s * rows, (s + 1) * rows)
        best[own, :], total[own, :], accum[own, :] = attend(
            q_rot[own, :], keys, values, None, None, None, causal
        )


def absorb(
    per_rank, count, fresh, last, info, q_rot, best_in, total_in, accum_in, *rest
):
    pieces, rest = rest[:count], rest[count:]
    rest = rest[0 if fresh else 1 :]
    if last:
        best, total, accum, context_ref, pages_ref, rows_out = rest[:6]
        rest = rest[6:]
    else:
        best, total, accum, pages_ref = rest[:4]
        rest = rest[4:]
    kv, page, where, page_sem, out_sem = rest
    tok = per_rank * SPAN
    rows = QH * SPAN
    block = 2 * tok + META

    blocks = [(p, base) for p in pieces for base in range(0, p.shape[0], block)]
    lane = lax.broadcasted_iota(jnp.int32, (META, HD), 1)
    slot = lax.broadcasted_iota(jnp.int32, (META, HD), 0)
    found = [jnp.int32(0)] * per_rank
    pages = [jnp.int32(0)] * per_rank
    group = 24 // per_rank
    for first in range(0, len(blocks), group):
        some = blocks[first : first + group]
        numbers = jnp.full((META, HD), -1.0, jnp.float32)
        for i, (piece, base) in enumerate(some):
            meta = piece[base + 2 * tok : base + block, :].astype(jnp.float32)
            numbers = jnp.where(lane == i, meta, numbers)
        numbers = numbers.astype(jnp.int32)
        valid = (slot < per_rank) & (lane < len(some))
        weight = jnp.left_shift(1, jnp.where(valid, lane * per_rank + slot, 0)).astype(jnp.float32)
        places = ((2 * (first + lane) * per_rank + slot) * SPAN + 1).astype(jnp.float32)

        def row(i):
            return info[i : i + 1, :]

        def choose(mask, x):
            return jnp.sum(jnp.where(mask & valid, x, 0.0)).astype(jnp.int32)

        bits = [choose((numbers >= row(s)) & (numbers < row(per_rank + s)), weight) for s in range(per_rank)]
        for p in range(per_rank):
            pages[p] = pages[p] + choose(numbers == row(2 * per_rank + p), places)
        for i in range(len(some)):
            for j in range(per_rank):
                for s in range(per_rank):
                    where[s, found[s]] = (2 * (first + i) * per_rank + j) * SPAN
                    found[s] = found[s] + (jnp.right_shift(bits[s], i * per_rank + j) & 1)

    for i, (piece, base) in enumerate(blocks):
        kv[2 * tok * i : 2 * tok * (i + 1), :] = piece[base : base + 2 * tok, :]

    def tile(place):
        return kv[pl.ds(pl.multiple_of(place, SPAN), SPAN), :]

    def page_copy(p):
        return pltpu.make_async_copy(page.at[p], pages_ref.at[p], page_sem.at[p])

    for p in range(per_rank):

        @pl.when(pages[p] > 0)
        def _():
            page[p, :, :HD] = tile(pages[p] - 1)
            page[p, :, HD:] = tile(pages[p] - 1 + tok)
            page_copy(p).start()

    def step(at, size, *slots):
        places = [[where[s, at[s] + i] for i in range(size)] for s in slots]
        own = slice(slots[0] * rows, (slots[-1] + 1) * rows)
        scores = jnp.concatenate(
            [
                scores_of(q_rot[s * rows : (s + 1) * rows, :], jnp.concatenate([tile(p) for p in some], axis=0))
                for s, some in zip(slots, places)
            ],
            axis=0,
        )
        old = best[own, :]
        top = jnp.maximum(old, jnp.max(scores, axis=1, keepdims=True))
        factor = jnp.exp2((old - top) * SCALE)
        weights = jnp.exp2((scores - jnp.tile(top, (1, size))) * SCALE)
        best[own, :] = top
        total[own, :] = total[own, :] * factor + lanes(weights, jnp.add)
        weights = weights.astype(jnp.bfloat16)
        accum[own, :] = accum[own, :] * factor + jnp.concatenate(
            [
                jnp.dot(
                    weights[i * rows : (i + 1) * rows, :],
                    jnp.concatenate([tile(p + tok) for p in some], axis=0),
                    preferred_element_type=jnp.float32,
                )
                for i, some in enumerate(places)
            ],
            axis=0,
        )

    def write(s):
        own = slice(s * SPAN, (s + 1) * SPAN)
        for h in range(QH):
            part = slice(s * rows + h * SPAN, s * rows + (h + 1) * SPAN)
            rows_out[own, h * HD : (h + 1) * HD] = (
                accum[part, :] / jnp.sum(total[part, :], axis=1, keepdims=True)
            ).astype(jnp.bfloat16)
        return pltpu.make_async_copy(rows_out.at[own, :], context_ref.at[own, :], out_sem.at[s])

    seen = found
    full = [n // LADDER for n in seen]
    shared = functools.reduce(jnp.minimum, full)
    everyone = tuple(range(per_rank))

    @pl.loop(0, shared)
    def _(b):
        step([LADDER * b] * per_rank, LADDER, *everyone)

    for s in everyone:

        @pl.loop(shared, full[s])
        def _(b):
            step([LADDER * b] * per_rank, LADDER, s)

    at = [LADDER * n for n in full]
    for size in range(LADDER - 1, 0, -1):
        want = [n % LADDER == size for n in seen]
        together = functools.reduce(jnp.logical_and, want)

        @pl.when(together)
        def _():
            step(at, size, *everyone)

        for s in everyone:

            @pl.when(want[s] & jnp.logical_not(together))
            def _():
                step(at, size, s)

    outs = []
    if last:
        for s in everyone:
            outs.append(write(s))
            outs[-1].start()

    for copy in outs:
        copy.wait()
    for p in range(per_rank):

        @pl.when(pages[p] > 0)
        def _():
            page_copy(p).wait()


SMEM = pl.BlockSpec(memory_space=pltpu.SMEM)
VMEM = pl.BlockSpec(memory_space=pltpu.VMEM)
ANY = pl.BlockSpec(memory_space=pltpu.HBM)
LIMIT = pltpu.CompilerParams(vmem_limit_bytes=24 << 20)


def vmem(x):
    return pltpu.with_memory_space_constraint(x, pltpu.VMEM)


def hbm(x):
    return pltpu.with_memory_space_constraint(x, pltpu.HBM)


ROUTE = (
    ("v1", "o", 8, 8),
    ("v2", "o", 2, 4),
    ("v3", "o", 4, 2),
    ("co", "o", 1, 1),
    ("v4", "v1", 2, 4),
    ("v5", "v1", 4, 2),
    ("v6", "v3", 2, 4),
    ("cv3", "v3", 1, 1),
    ("cv1", "v1", 1, 1),
    ("cv2", "v2", 1, 1),
    ("v7", "v4", 4, 2),
    ("cv4", "v4", 1, 1),
    ("cv5", "v5", 1, 1),
    ("cv6", "v6", 1, 1),
    ("cv7", "v7", 1, 1),
)
SOON = ("o", "v1", "v2", "v3", "co", "cv1", "cv2", "cv3", "v4", "cv4", "v5")
MID = ("v6", "cv5", "v7")
LATE = ("cv6", "cv7")


def on_device(ranks, queries, keys, values, span_ids, lengths, page_dest):
    return plan(ranks, queries, keys, values, span_ids, lengths, page_dest)


def plan(ranks, queries, keys, values, span_ids, lengths, page_dest):
    tok = queries.shape[0]
    per_rank = span_ids.shape[0]
    spans = page_dest.shape[0]
    block = 2 * tok + META
    rows = per_rank * QH * SPAN
    cosine, sine = (jnp.asarray(t) for t in tables(spans))
    ints = [pltpu.SMEM(x.shape, x.dtype) for x in (span_ids, lengths)]
    turns = [pltpu.VMEM(x.shape, x.dtype) for x in (cosine, sine)]
    packed = pl.pallas_call(
        functools.partial(prepare, spans),
        out_shape=pltpu.VMEM((block, HD), jnp.bfloat16),
        in_specs=[ANY] * 6,
        out_specs=VMEM,
        scratch_shapes=ints
        + [pltpu.VMEM(x.shape, x.dtype) for x in (keys, values)]
        + turns
        + [pltpu.SemaphoreType.DMA((6,))],
        compiler_params=LIMIT,
        name="prepare",
    )(*map(hbm, (span_ids, lengths, keys, values, cosine, sine)))

    def swap(x, even, odd):
        return lax.ppermute(x, "seq", [(i, i ^ (odd if i % 2 else even)) for i in range(ranks)])

    own = packed
    distance = ranks // 2
    while distance >= 16:
        own = jnp.concatenate([own, swap(own, distance, distance)], axis=0)
        distance //= 2
    held = {"o": own}
    for name, source, even, odd in ROUTE:
        held[name] = swap(held[source], even, odd)

    state_shapes = tuple(pltpu.VMEM((rows, n), jnp.float32) for n in (HD, HD, HD))
    info, q_rot, *state = pl.pallas_call(
        functools.partial(early, spans),
        out_shape=(
            pltpu.VMEM((-(-3 * per_rank // 8) * 8, HD), jnp.int32),
            pltpu.VMEM((rows, HD), jnp.bfloat16),
            *state_shapes,
        ),
        in_specs=[ANY] * 6 + [VMEM],
        out_specs=(VMEM,) * 5,
        scratch_shapes=ints
        + [pltpu.SMEM(page_dest.shape, page_dest.dtype), pltpu.VMEM(queries.shape, queries.dtype)]
        + turns
        + [pltpu.SemaphoreType.DMA((6,))],
        compiler_params=LIMIT,
        name="early",
    )(*map(hbm, (span_ids, lengths, page_dest, queries, cosine, sine)), vmem(packed))

    pages_shape = jax.ShapeDtypeStruct((per_rank, SPAN, 2 * HD), jnp.bfloat16)

    def take(names, state, pages, last=False):
        pieces = [vmem(held[n]) for n in names]
        length = sum(p.shape[0] for p in pieces)
        units = length // block
        scratch = [
            pltpu.VMEM((units * 2 * tok, HD), jnp.bfloat16),
            pltpu.VMEM((per_rank, SPAN, 2 * HD), jnp.bfloat16),
            pltpu.SMEM((per_rank, units * per_rank + 4), jnp.int32),
            pltpu.SemaphoreType.DMA((per_rank,)),
            pltpu.SemaphoreType.DMA((per_rank,)),
        ]
        if last:
            context_shape = jax.ShapeDtypeStruct((tok, QH * HD), jnp.bfloat16)
            out_shape = (*state_shapes, context_shape, pages_shape)
            out_specs = (VMEM,) * 3 + (ANY, ANY)
            scratch = [pltpu.VMEM((tok, QH * HD), jnp.bfloat16)] + scratch
        else:
            out_shape = (*state_shapes, pages_shape)
            out_specs = (VMEM,) * 3 + (ANY,)
        inputs = [vmem(info), vmem(q_rot), *map(vmem, state), *pieces]
        in_specs = [VMEM] * (5 + len(pieces))
        aliases = {2: 0, 3: 1, 4: 2}
        if pages is not None:
            aliases[len(inputs)] = len(out_shape) - 1
            inputs.append(pages)
            in_specs.append(ANY)
        return pl.pallas_call(
            functools.partial(absorb, per_rank, len(pieces), pages is None, last),
            out_shape=out_shape,
            in_specs=in_specs,
            out_specs=out_specs,
            scratch_shapes=scratch,
            input_output_aliases=aliases,
            compiler_params=LIMIT,
        )(*inputs)

    *state, pages = take(SOON, state, None)
    *state, pages = take(MID, state, pages)
    *_, context, pages = take(LATE, state, pages, last=True)
    return context, pages


def solution(mesh):
    return jax.shard_map(
        functools.partial(on_device, mesh.shape["seq"]),
        mesh=mesh,
        in_specs=(
            P(("groups", "seq"), None),
            P(("groups", "seq"), None),
            P(("groups", "seq"), None),
            P(("groups", "seq")),
            P("groups"),
            P("groups"),
        ),
        out_specs=(P(("groups", "seq"), None), P(("groups", "seq"), None, None)),
        check_vma=False,
    )
```
